32 devices in a mesh: rep: 2 (over y), grp: 8 (over z, x), sub: 2 (over core).
Axes of the slice: x: 2, y: 2, z: 4, core: 2. Of those that a mesh axis runs over, the one named last changes fastest.
Arguments:
- query_rows: bfloat16 [16, 4, 5120], P(('grp', 'sub'), 'rep'), parts along dimension 1, may hold values from -120 to 120
- cache_keys: bfloat16 [16, 4, 128, 1024], P(('grp', 'sub'), 'rep'), parts along dimension 1, may hold values from -6 to 6
- cache_values: bfloat16 [16, 4, 128, 1024], P(('grp', 'sub'), 'rep'), parts along dimension 1, may hold values from -6 to 6
- residual: bfloat16 [16, 4, 5120], P(('grp', 'sub'), 'rep'), parts along dimension 1, may hold values from -6 to 6
- lengths: int32 [16, 4], P(('grp', 'sub'), 'rep'), parts along dimension 1, may hold values from 3 to 128
- expert_ids: int32 [16, 4, 1], P(('grp', 'sub'), 'rep'), parts along dimension 1, may hold values from 0 to 3; in each aligned block of 2 rows (0 to 1, 2 to 3, ..., all dimensions but the last counted through in order) at most 2 rows name the same one
- capacity: int32 [4], replicated, may hold values from 1 to 2
- norm_gain: float32 [5120], replicated, may hold values from 0.5 to 1.5
- router: bfloat16 [5120, 4], replicated, may hold values from -0.078125 to 0.078125
- shared_gate: bfloat16 [5120, 8192], P(None, ('grp', 'sub')), may hold values from -0.078125 to 0.078125
- shared_up: bfloat16 [5120, 8192], P(None, ('grp', 'sub')), may hold values from -0.078125 to 0.078125
- shared_down: bfloat16 [8192, 5120], P(('grp', 'sub')), may hold values from -0.0625 to 0.0625
- expert_gate: bfloat16 [5120, 32768], P(None, ('grp', 'sub')), may hold values from -0.078125 to 0.078125
- expert_up: bfloat16 [5120, 32768], P(None, ('grp', 'sub')), may hold values from -0.078125 to 0.078125
- expert_down: bfloat16 [32768, 5120], P(('grp', 'sub')), may hold values from -0.0625 to 0.0625
Outputs:
- layer_out: bfloat16 [16, 4, 5120], P(('grp', 'sub'), 'rep'), parts along dimension 1
The draws below stay inside these ranges and needn't reach their ends.
There are 2 independent parts, one for each index of `rep`. The reference program is written for one: setup_inputs(seed, part) draws one part's arguments, and reference() takes and returns one part's arrays. A program takes and returns all parts, laid end to end along the dimension named above; an argument that names none is the same for every part. Nothing has to cross between parts.
Inputs may be any that keep to these rules, and one draw needn't show every extreme that they name: `expert_ids`: in each aligned block of 2 rows (the rows of one device), no expert is named more than 2 times.
All inputs are finite; a program needn't handle non-finite values.
Results may differ from the reference program's by a relative error of at most 0.0075.
Values may be sent and summed in bfloat16 or wider, within the bound.
A program may use at most 128 MiB of HBM per device.

```python
import math
import jax
import jax.numpy as jnp
import numpy as np
from jax import lax

D = 5120
HEADS = 40
KV_HEADS = 8
HEAD = 128
EXPERTS = 4
EH = 8192
SH = 8192
CTX = 128
REQ_DEV = 2
HOLDERS = 16
CAP = 2


def query_key_pair(key):
    base_key = jax.random.fold_in(key, 91)
    key_part = jnp.clip(jax.random.normal(jax.random.fold_in(base_key, 1), (HOLDERS, REQ_DEV, CTX, KV_HEADS * HEAD), jnp.float32), -6.0, 6.0)
    query_part = jnp.clip(jax.random.normal(jax.random.fold_in(base_key, 2), (HOLDERS, REQ_DEV, HEADS * HEAD), jnp.float32), -6.0, 6.0)
    return (query_part, key_part)


def draw_query_rows(key, part):
    query_part, key_part = query_key_pair(key)
    return query_part.astype(jnp.bfloat16)


def draw_cache_keys(key, part):
    query_part, key_part = query_key_pair(key)
    return key_part.astype(jnp.bfloat16)


def plant(values, key, low, largest):
    spot = [jax.random.randint(jax.random.fold_in(key, axis), (), 0, length) for axis, length in enumerate(values.shape)]
    longest = values.shape.index(max(values.shape))
    beside = spot[:longest] + [(spot[longest] + 1) % values.shape[longest]] + spot[longest + 1:]
    return values.at[tuple(spot)].set(low).at[tuple(beside)].set(largest)


def shard_levels(key, shape, split, least, high):
    def one(dim, shards_of):
        steps = jax.random.uniform(jax.random.fold_in(jax.random.fold_in(key, 6), dim), (shards_of,), jnp.float32, least / len(split), high / len(split))
        return jnp.repeat(jnp.exp(steps), shape[dim] // shards_of).reshape((-1,) + (1,) * (len(shape) - dim - 1))

    factor_of = one(*split[0])
    for cut in split[1:]:
        factor_of = factor_of * one(*cut)
    return factor_of


def deal_out(key, own, number, rows, count, top, limit, slope):
    order = jax.random.permutation(key, count)
    heavy_load, ordinary = portions_of(count, rows * top, limit, slope, True), portions_of(count, rows * top, limit, slope, False)
    places = jnp.arange(count)

    def named(sizes, rotation):
        used = int((sizes > 0).sum())
        fixed = max(1, used // 4)
        moved = fixed + (places - fixed + rotation * (used - fixed)) % max(1, count - fixed)
        return jnp.zeros((count,), jnp.int32).at[order[jnp.where(places < fixed, places, moved)]].set(jnp.asarray(sizes, jnp.int32))

    sizes = jnp.where(number % 4 == 0, named(heavy_load, number // 4), named(ordinary, number - number // 4 - 1))
    mixed = jax.random.permutation(jax.random.fold_in(own, 3), count)
    giver, sink = mixed[0:count // 2 * 2:2], mixed[1:count // 2 * 2:2]
    margin = jnp.minimum(sizes[giver] - 1, limit - sizes[sink]) // 2
    margin = jnp.where((giver == order[0]) | (sink == order[0]) | (sizes[sink] == 0), 0, jnp.maximum(margin, 0))
    moved = jax.random.randint(jax.random.fold_in(own, 4), (count // 2,), 0, 1 << 20) % (margin + 1)
    sizes = sizes.at[giver].add(-moved).at[sink].add(moved)
    labels = jnp.searchsorted(jnp.cumsum(sizes), jnp.arange(rows * top), side="right").astype(jnp.int32)
    grid = labels.reshape(top, rows).T
    grid = grid[jax.random.permutation(jax.random.fold_in(own, 1), rows)]
    rotation = jax.random.randint(jax.random.fold_in(own, 2), (rows, 1), 0, top)
    return jnp.take_along_axis(grid, (jnp.arange(top)[None, :] + rotation) % top, axis=1)


def portions_of(number_of, total, reach, skew, full):
    portions = [(1 << 20) // math.isqrt(standing ** skew) + 1 for standing in range(1, number_of + 1)]
    largest = reach if full else min(reach, max(-(-total // number_of), total * portions[0] // sum(portions)))
    least = 1 if total - largest >= number_of - 1 else 0
    counts, surplus = [largest] + [least] * (number_of - 1), total - largest - least * (number_of - 1)
    while surplus > 0:
        free = [i for i in range(1, number_of) if counts[i] < largest] or [i for i in range(1, number_of) if counts[i] < reach]
        pool, budget = sum([portions[i] for i in free]), surplus
        for i in free:
            addition = min(reach - counts[i], max(1, budget * portions[i] // pool), surplus)
            counts[i] = counts[i] + addition
            surplus = surplus - addition
    return np.array(counts)


def centred(key, extent, deviation, reach, cuts=(), kind=jnp.bfloat16):
    drawn = jax.random.normal(key, extent, jnp.float32) * deviation
    if len(cuts) > 0:
        drawn = shard_levels(key, extent, cuts, -0.22, 0.18) * drawn
    return jnp.clip(drawn, min=-reach, max=reach).astype(kind)


def setup_inputs(seed: int = 0, part: int = 0) -> dict:
    keys = jax.random.split(jax.random.key(seed), 16)
    part_splits = jax.random.split(jax.random.fold_in(keys[15], part), 16)
    query_rows = draw_query_rows(jax.random.fold_in(jax.random.fold_in(keys[15], part), 71), part)
    cache_keys = draw_cache_keys(jax.random.fold_in(jax.random.fold_in(keys[15], part), 71), part)
    cache_values = centred(part_splits[2], (HOLDERS, REQ_DEV, CTX, KV_HEADS * HEAD), 1.0, 6.0, ((0, 16),))
    residual = centred(part_splits[3], (HOLDERS, REQ_DEV, D), 1.0, 6.0, ((0, 16),))
    lengths = plant(jax.random.randint(part_splits[4], (HOLDERS, REQ_DEV), 3, CTX + 1), jax.random.fold_in(part_splits[4], 1), 3, CTX).astype(jnp.int32)
    expert_ids_keys = jax.random.split(jax.random.fold_in(part_splits[5], 1), HOLDERS * REQ_DEV // REQ_DEV)
    expert_ids_turns = jax.random.permutation(jax.random.fold_in(part_splits[5], 3), HOLDERS * REQ_DEV // REQ_DEV)
    expert_ids = jax.vmap(lambda own, number: deal_out(jax.random.fold_in(part_splits[5], 2), own, number, REQ_DEV, EXPERTS, 1, CAP, 2))(expert_ids_keys, expert_ids_turns).reshape((HOLDERS, REQ_DEV, 1))
    capacity = plant(jax.random.randint(keys[6], (EXPERTS,), max(1, CAP // 2), CAP + 1), jax.random.fold_in(keys[6], 1), max(1, CAP // 2), CAP).astype(jnp.int32)
    norm_gain = jnp.clip(1.0 + 0.1 * jax.random.normal(keys[7], (D,), jnp.float32), 0.5, 1.5)
    router = centred(keys[8], (D, EXPERTS), D ** -0.5, 0.078125)
    shared_gate = centred(keys[9], (D, SH), D ** -0.5, 0.078125, ((1, 16),))
    shared_up = centred(keys[10], (D, SH), D ** -0.5, 0.078125, ((1, 16),))
    shared_down = centred(keys[11], (SH, D), SH ** -0.5, 0.0625, ((0, 16),))
    expert_gate = centred(keys[12], (D, EXPERTS * EH), D ** -0.5, 0.078125, ((1, 16),))
    expert_up = centred(keys[13], (D, EXPERTS * EH), D ** -0.5, 0.078125, ((1, 16),))
    expert_down = centred(keys[14], (EXPERTS * EH, D), EH ** -0.5, 0.0625, ((0, 16),))
    return dict(query_rows=query_rows, cache_keys=cache_keys, cache_values=cache_values, residual=residual, lengths=lengths, expert_ids=expert_ids, capacity=capacity, norm_gain=norm_gain, router=router, shared_gate=shared_gate, shared_up=shared_up, shared_down=shared_down, expert_gate=expert_gate, expert_up=expert_up, expert_down=expert_down)


def attend(query_rows, cache_keys, cache_values, lengths):
    request_count = query_rows.shape[0]
    groups = HEADS // KV_HEADS
    queries_f = query_rows.astype(jnp.float32).reshape(request_count, KV_HEADS, groups, HEAD)
    keys_f = cache_keys.astype(jnp.float32).reshape(request_count, CTX, KV_HEADS, HEAD)
    scores = jnp.einsum('rkgh,rjkh->rkgj', queries_f, keys_f) * HEAD ** (-0.5)
    key_pos = jnp.arange(CTX, dtype=jnp.int32)
    allowed = (key_pos[None, :] < lengths[:, None])[:, None, None, :]
    scores = jnp.where(allowed, scores, -1e+30)
    row_peak = lax.optimization_barrier(jnp.max(scores, axis=-1, keepdims=True))
    exponent = jnp.where(allowed, jnp.exp(scores - row_peak), 0.0)
    weights = (exponent / lax.optimization_barrier(jnp.sum(exponent, axis=-1, keepdims=True))).astype(jnp.bfloat16)
    values_f = cache_values.astype(jnp.float32).reshape(request_count, CTX, KV_HEADS, HEAD)
    attended = jnp.einsum('rkgj,rjkh->rkgh', weights.astype(jnp.float32), values_f)
    return attended.reshape(request_count, HEADS * HEAD).astype(jnp.bfloat16)

def rms_normalize(stream, norm_gain):
    mean_square = lax.optimization_barrier(jnp.mean(stream * stream, axis=-1, keepdims=True))
    return (stream * lax.rsqrt(mean_square + 1e-05) * norm_gain).astype(jnp.bfloat16)

def swiglu(inputs, w_gate, w_up, w_down):
    gate_part = jnp.dot(inputs, w_gate, preferred_element_type=jnp.float32)
    up_part = jnp.dot(inputs, w_up, preferred_element_type=jnp.float32)
    hidden = (jax.nn.silu(gate_part) * up_part).astype(jnp.bfloat16)
    return jnp.dot(hidden, w_down, preferred_element_type=jnp.float32)

def gated_inputs(flat_rows, router, route_ids):
    logits = jnp.dot(flat_rows, router, preferred_element_type=jnp.float32)
    onehot = route_ids[:, None] == jnp.arange(EXPERTS, dtype=jnp.int32)[None, :]
    picked = lax.optimization_barrier(jnp.sum(jnp.where(onehot, logits, 0.0), axis=-1))
    return (flat_rows.astype(jnp.float32) * jax.nn.sigmoid(picked)[:, None]).astype(jnp.bfloat16)

def build_slots(route_ids, capacity):
    onehot = (route_ids[:, None] == jnp.arange(EXPERTS, dtype=jnp.int32)[None, :]).astype(jnp.int32)
    before = jnp.cumsum(onehot, axis=0) - onehot
    row_rank = lax.optimization_barrier(jnp.sum(before * onehot, axis=1))
    row_limit = lax.optimization_barrier(jnp.sum(onehot * capacity[None, :], axis=1))
    kept_rows = row_rank < row_limit
    expert_match = route_ids[None, None, :] == jnp.arange(EXPERTS, dtype=jnp.int32)[:, None, None]
    slot_match = row_rank[None, None, :] == jnp.arange(CAP, dtype=jnp.int32)[None, :, None]
    return (expert_match & slot_match & kept_rows[None, None, :]).astype(jnp.float32)

def reference(query_rows, cache_keys, cache_values, residual, lengths, expert_ids, capacity, norm_gain, router, shared_gate, shared_up, shared_down, expert_gate, expert_up, expert_down):
    row_count = HOLDERS * REQ_DEV
    attended = attend(query_rows.reshape(row_count, HEADS * HEAD), cache_keys.reshape(row_count, CTX, KV_HEADS * HEAD), cache_values.reshape(row_count, CTX, KV_HEADS * HEAD), lengths.reshape(row_count))
    stream = residual.reshape(row_count, D).astype(jnp.float32) + attended.astype(jnp.float32)
    flat_rows = rms_normalize(stream, norm_gain)
    shared_out = swiglu(flat_rows, shared_gate, shared_up, shared_down)
    route_ids = expert_ids.reshape(row_count)
    scaled = gated_inputs(flat_rows, router, route_ids)
    blocks = HOLDERS
    selection = jax.vmap(build_slots, in_axes=(0, None))(route_ids.reshape(blocks, REQ_DEV), capacity)
    slot_rows = jnp.einsum('becr,brd->ebcd', selection, scaled.reshape(blocks, REQ_DEV, D).astype(jnp.float32))
    slot_rows = slot_rows.astype(jnp.bfloat16).reshape(EXPERTS, blocks * CAP, D)

    def one_expert(packed):
        expert_index, inputs = packed
        start_col = expert_index * EH
        w_gate = lax.dynamic_slice_in_dim(expert_gate, start_col, EH, 1)
        w_up = lax.dynamic_slice_in_dim(expert_up, start_col, EH, 1)
        w_down = lax.dynamic_slice_in_dim(expert_down, start_col, EH, 0)
        return swiglu(inputs, w_gate, w_up, w_down)
    expert_out = lax.map(one_expert, (jnp.arange(EXPERTS, dtype=jnp.int32), slot_rows))
    routed = jnp.einsum('becr,ebcd->brd', selection, expert_out.reshape(EXPERTS, blocks, CAP, D))
    layer_out = stream + shared_out + routed.reshape(row_count, D)
    return layer_out.astype(jnp.bfloat16).reshape(HOLDERS, REQ_DEV, D)
```

```python
import functools

import jax
import jax.numpy as jnp
from jax import lax
from jax.experimental import pallas as pl
from jax.experimental.pallas import tpu as pltpu
from jax.sharding import PartitionSpec as P

D = 5120
HEADS = 40
KV_HEADS = 8
HEAD = 128
EXPERTS = 4
EH = 8192


def attend(query_rows, cache_keys, cache_values, lengths):
    request_count = query_rows.shape[0]
    context = cache_keys.shape[1]
    groups = HEADS // KV_HEADS
    queries_f = query_rows.astype(jnp.float32).reshape(request_count, KV_HEADS, groups, HEAD)
    keys_f = cache_keys.astype(jnp.float32).reshape(request_count, context, KV_HEADS, HEAD)
    scores = jnp.einsum("rkgh,rjkh->rkgj", queries_f, keys_f) * HEAD ** (-0.5)
    key_pos = jnp.arange(context, dtype=jnp.int32)
    allowed = (key_pos[None, :] < lengths[:, None])[:, None, None, :]
    scores = jnp.where(allowed, scores, -1e30)
    row_peak = jnp.max(scores, axis=-1, keepdims=True)
    exponent = jnp.where(allowed, jnp.exp(scores - row_peak), 0.0)
    weights = (exponent / jnp.sum(exponent, axis=-1, keepdims=True)).astype(jnp.bfloat16)
    values_f = cache_values.astype(jnp.float32).reshape(request_count, context, KV_HEADS, HEAD)
    attended = jnp.einsum("rkgj,rjkh->rkgh", weights.astype(jnp.float32), values_f)
    return attended.reshape(request_count, HEADS * HEAD).astype(jnp.bfloat16)


def rms_normalize(stream, norm_gain):
    mean_square = jnp.mean(stream * stream, axis=-1, keepdims=True)
    return (stream * lax.rsqrt(mean_square + 1e-05) * norm_gain).astype(jnp.bfloat16)


def swiglu(inputs, w_gate, w_up, w_down):
    gate_part = jnp.dot(inputs, w_gate, preferred_element_type=jnp.float32)
    up_part = jnp.dot(inputs, w_up, preferred_element_type=jnp.float32)
    hidden = (jax.nn.silu(gate_part) * up_part).astype(jnp.bfloat16)
    return jnp.dot(hidden, w_down, preferred_element_type=jnp.float32)


def gated_inputs(flat_rows, router, route_ids):
    logits = jnp.dot(flat_rows, router, preferred_element_type=jnp.float32)
    onehot = route_ids[:, None] == jnp.arange(EXPERTS, dtype=jnp.int32)[None, :]
    picked = jnp.sum(jnp.where(onehot, logits, 0.0), axis=-1)
    return (flat_rows.astype(jnp.float32) * jax.nn.sigmoid(picked)[:, None]).astype(jnp.bfloat16)


def row_ranks(route_ids, capacity):
    onehot = (route_ids[:, None] == jnp.arange(EXPERTS, dtype=jnp.int32)[None, :]).astype(jnp.int32)
    before = jnp.cumsum(onehot, axis=0) - onehot
    row_rank = jnp.sum(before * onehot, axis=1)
    row_limit = jnp.sum(onehot * capacity[None, :], axis=1)
    return (row_rank, row_rank < row_limit)


def per_device(
    query_rows,
    cache_keys,
    cache_values,
    residual,
    lengths,
    expert_ids,
    capacity,
    norm_gain,
    router,
    shared_gate,
    shared_up,
    shared_down,
    expert_gate,
    expert_up,
    expert_down,
):
    tok_count = query_rows.shape[1]
    attended = attend(query_rows[0], cache_keys[0], cache_values[0], lengths[0])
    stream = residual[0].astype(jnp.float32) + attended.astype(jnp.float32)
    flat_rows = rms_normalize(stream, norm_gain)
    route_ids = expert_ids[0].reshape(tok_count)
    gathered, all_ids = (
        lax.all_gather(flat_rows, ("grp", "sub"), axis=0, tiled=True),
        lax.all_gather(route_ids, ("grp", "sub"), axis=0, tiled=True),
    )
    all_scaled = gated_inputs(gathered, router, all_ids)
    rank_unused, kept_all = jax.vmap(row_ranks, in_axes=(0, None))(
        all_ids.reshape(-1, tok_count), capacity
    )
    own_expert = lax.axis_index(("grp", "sub")) * expert_gate.shape[1] // EH
    usable = (all_ids == own_expert) & kept_all.reshape(-1)
    masked = jnp.where(usable[:, None], all_scaled, jnp.zeros_like(all_scaled))
    shared_part = swiglu(gathered, shared_gate, shared_up, shared_down)
    branch_sum = lax.psum_scatter(
        shared_part + swiglu(masked, expert_gate, expert_up, expert_down),
        ("grp", "sub"),
        scatter_dimension=0,
        tiled=True,
    )
    layer_out = stream + branch_sum
    return layer_out.astype(jnp.bfloat16).reshape(1, tok_count, D)


def fused_layer(sizes, *refs):
    (q_in, k_in, v_in, res_in, len_in, ids_in, cap_in, gain_in, router_in,
     sg_in, su_in, sd_in, eg_in, eu_in, ed_in, out_ref,
     slots, q_raw, res_raw, router_raw, gain_v, len_s, ids_s, cap_s,
     rows_a, rows_b, stream_v, router_f, gathered, gates, gathered_f, x_v, hidden, gate_part,
     stage, own_part, send_buf, recv_buf,
     small_sem, kv_sem, a_sem, b_sem, gs_sem, gr_sem, ts_sem, tr_sem, rs_sem, rr_sem) = refs
    subs, peers, tok = sizes
    width = slots.shape[2]
    depth = slots.shape[1]
    slot_count = slots.shape[0]
    lanes = 128
    heads = D // lanes
    groups = HEADS // KV_HEADS
    context = k_in.shape[2]
    shared_w, expert_w = sg_in.shape[1], eg_in.shape[1]
    pairs = 1 + expert_w // width
    half = depth // 2
    down_rows = shared_w + expert_w
    chunk = 2 * width
    chunks = D // chunk
    tiles = chunk // lanes
    total = peers * tok
    f32, bf16 = jnp.float32, jnp.bfloat16

    rep = lax.axis_index("rep")
    me = lax.axis_index("grp") * subs + lax.axis_index("sub")

    def device(p):
        return (rep, p // subs, p % subs)

    small = [
        pltpu.make_async_copy(src, dst, small_sem.at[i])
        for i, (src, dst) in enumerate((
            (q_in, q_raw), (res_in, res_raw), (len_in, len_s), (ids_in, ids_s),
            (cap_in, cap_s), (gain_in, gain_v), (router_in, router_raw)))
    ]
    for copy in small:
        copy.start()

    kv_slot = slot_count - 1
    kv_cols = KV_HEADS * HEAD // width
    kv_copies = []
    for which, ref in enumerate((k_in, v_in)):
        for r in range(tok):
            for b in range(kv_cols):
                at = ((which * tok + r) * kv_cols + b)
                copy = pltpu.make_async_copy(
                    ref.at[0, r, :, pl.ds(b * width, width)],
                    slots.at[kv_slot, pl.ds(at * context, context), :],
                    kv_sem.at[at])
                copy.start()
                kv_copies.append(copy)

    def a_copy(s, h):
        p, up = s // 2, s % 2
        rows = pl.ds(h * half, half)
        if p == 0:
            src = (su_in if up else sg_in).at[rows, :]
        else:
            src = (eu_in if up else eg_in).at[rows, pl.ds((p - 1) * width, width)]
        return pltpu.make_async_copy(src, slots.at[s, rows, :], a_sem.at[s, h])

    def b_slot(j):
        return lax.rem(2 * pairs + j, slot_count)

    def b_start(j):
        s = (2 * pairs + j) % slot_count
        for h in range(2):
            cols = pl.ds(j * chunk + h * width, width)
            pltpu.make_async_copy(
                sd_in.at[:, cols], slots.at[s, pl.ds(h * down_rows, shared_w), :],
                b_sem.at[j, h, 0]).start()
            pltpu.make_async_copy(
                ed_in.at[:, cols], slots.at[s, pl.ds(h * down_rows + shared_w, expert_w), :],
                b_sem.at[j, h, 1]).start()

    for s in range(2 * pairs):
        for h in range(2):
            a_copy(s, h).start()
    ahead = slot_count - 1 - 2 * pairs
    for j in range(ahead):
        b_start(j)

    barrier = pltpu.get_barrier_semaphore()

    def greet(k, carry):
        pl.semaphore_signal(barrier, inc=1, device_id=device(lax.rem(me + k, peers)),
                            device_id_type=pl.DeviceIdType.MESH)
        return carry

    lax.fori_loop(1, peers, greet, 0)

    for copy in small:
        copy.wait()
    rows_a[...] = jnp.zeros_like(rows_a)
    for c in range(heads):
        cols = pl.ds(c * lanes, lanes)
        rows_a[pl.ds(c, tok, stride=heads), :] = q_raw[0, :, cols].astype(f32)
        stream_v[pl.ds(c, tok, stride=heads), :] = res_raw[0, :, cols].astype(f32)
        router_f[pl.ds(c, EXPERTS, stride=heads), :] = router_raw[:, cols].astype(f32)
    for copy in kv_copies:
        copy.wait()

    def cache(which, r, g):
        b, inner = divmod(g * HEAD, width)
        at = (which * tok + r) * kv_cols + b
        return slots[kv_slot, at * context:(at + 1) * context, inner:inner + HEAD]

    for r in range(tok):
        for g in range(KV_HEADS):
            at = r * heads + g * groups
            rows_b[at:at + 8, :] = lax.dot_general(
                rows_a[at:at + 8, :].astype(bf16), cache(0, r, g),
                (((1,), (1,)), ((), ())), preferred_element_type=f32)
    scores = rows_b[0:tok * heads, :] * HEAD ** (-0.5)
    row_of = lax.broadcasted_iota(jnp.int32, scores.shape, 0)
    limit = jnp.full(scores.shape, len_s[0, 0], jnp.int32)
    for r in range(1, tok):
        limit = jnp.where(row_of >= r * heads, len_s[0, r], limit)
    allowed = lax.broadcasted_iota(jnp.int32, scores.shape, 1) < limit
    scores = jnp.where(allowed, scores, -1e30)
    exponent = jnp.where(allowed, jnp.exp(scores - jnp.max(scores, axis=1, keepdims=True)), 0.0)
    rows_a[0:tok * heads, :] = exponent / jnp.sum(exponent, axis=1, keepdims=True)
    for r in range(tok):
        for g in range(KV_HEADS):
            at = r * heads + g * groups
            rows_b[at:at + 8, :] = jnp.dot(
                rows_a[at:at + 8, :].astype(bf16), cache(1, r, g), preferred_element_type=f32)
    for j in range(ahead, min(ahead + 1, chunks)):
        b_start(j)
    stream = stream_v[...] + rows_b[0:tok * heads, :].astype(bf16).astype(f32)
    stream_v[...] = stream
    ids = [ids_s[0, r] for r in range(tok)]
    normed_rows = []
    for r in range(tok):
        part = stream[r * heads:(r + 1) * heads, :]
        square = jnp.sum(jnp.sum(part * part, axis=0, keepdims=True), axis=1, keepdims=True) / D
        normed_rows.append((part * lax.rsqrt(square + 1e-05) * gain_v[...]).astype(bf16))
    gathered[me] = jnp.concatenate([n.astype(f32) for n in normed_rows], axis=0).astype(bf16)
    gate_rows = []
    for r in range(tok):
        normed_f = normed_rows[r].astype(f32)
        picked = jnp.zeros((1, 1), f32)
        row_limit = jnp.int32(0)
        for e in range(EXPERTS):
            prod = normed_f * router_f[e * heads:(e + 1) * heads, :]
            logit = jnp.sum(jnp.sum(prod, axis=0, keepdims=True), axis=1, keepdims=True)
            match = (ids[r] == e).astype(jnp.int32)
            picked = picked + logit * match.astype(f32)
            row_limit = row_limit + match * cap_s[e]
        rank = jnp.int32(0)
        for b in range(r):
            rank = rank + (ids[b] == ids[r]).astype(jnp.int32)
        kept = (rank < row_limit).astype(jnp.int32)
        sig = jnp.broadcast_to(1.0 / (1.0 + jnp.exp(-picked)), (1, lanes))
        for e in range(EXPERTS):
            gate_rows.append(sig * (kept * (ids[r] == e).astype(jnp.int32)).astype(f32))
    gate_tile = jnp.concatenate(gate_rows, axis=0)
    gates[me] = gate_tile

    pl.semaphore_wait(barrier, peers - 1)

    def remote(src, dst, ssem, rsem, p):
        return pltpu.make_async_remote_copy(
            src_ref=src, dst_ref=dst, send_sem=ssem, recv_sem=rsem,
            device_id=device(p), device_id_type=pl.DeviceIdType.MESH)

    def spread(k, carry):
        p = lax.rem(me + k, peers)
        remote(gathered.at[me], gathered.at[me], gs_sem.at[p], gr_sem.at[me], p).start()
        remote(gates.at[me], gates.at[me], ts_sem.at[p], tr_sem.at[me], p).start()
        return carry

    lax.fori_loop(1, peers, spread, 0)
    rows_per = tok * heads
    gathered_f[pl.ds(pl.multiple_of(me * rows_per, 8), rows_per), :] = gathered[me].astype(f32)

    def collect(k, carry):
        p = lax.rem(me + peers - k, peers)
        remote(gathered.at[p], gathered.at[p], gs_sem.at[p], gr_sem.at[p], p).wait_recv()
        remote(gates.at[p], gates.at[p], ts_sem.at[p], tr_sem.at[p], p).wait_recv()
        gathered_f[pl.ds(pl.multiple_of(p * rows_per, 8), rows_per), :] = gathered[p].astype(f32)
        return carry

    lax.fori_loop(1, peers, collect, 0)

    own_expert = me * expert_w // EH
    gate_all = gates[...].reshape(peers * tok * EXPERTS, lanes)
    stage[0:peers * tok * EXPERTS, :] = gate_all
    gate = jnp.zeros((total, lanes), f32)
    for e in range(EXPERTS):
        mine = (own_expert == e).astype(f32)
        gate = gate + mine * stage[pl.ds(e, total, stride=EXPERTS), :]
    for c in range(heads):
        piece = gathered_f[pl.ds(c, total, stride=heads), :]
        x_v[0, :, c * lanes:(c + 1) * lanes] = piece.astype(bf16)
        x_v[1, :, c * lanes:(c + 1) * lanes] = (piece * gate).astype(bf16)

    def a_wait(s, h):
        view = slots.at[s, pl.ds(h * half, half), :]
        pltpu.make_async_copy(view, view, a_sem.at[s, h]).wait()

    def up_dot(s, which):
        a_wait(s, 0)
        first = jnp.dot(x_v[which, :, 0:half], slots[s, 0:half, :], preferred_element_type=f32)
        a_wait(s, 1)
        return first + jnp.dot(x_v[which, :, half:depth], slots[s, half:depth, :],
                               preferred_element_type=f32)

    def up_pair(p, carry):
        which = jnp.minimum(p, 1)
        gate_part[...] = up_dot(2 * p, which)
        up = up_dot(2 * p + 1, which)
        g = gate_part[...]
        hidden[:, pl.ds(pl.multiple_of(p * width, width), width)] = (
            g / (1.0 + jnp.exp(-g)) * up).astype(bf16)
        return carry

    issued = ahead + 1
    done = 0
    while issued < chunks:
        up_pair(done, 0)
        done += 1
        for j in range(issued, min(issued + 2, chunks)):
            b_start(j)
        issued = min(issued + 2, chunks)
    lax.fori_loop(done, pairs, up_pair, 0)

    def down(j, carry):
        s = b_slot(j)
        for h in range(2):
            view = slots.at[s, pl.ds(h * down_rows, shared_w), :]
            pltpu.make_async_copy(view, view, b_sem.at[j, h, 0]).wait()
            view = slots.at[s, pl.ds(h * down_rows + shared_w, expert_w), :]
            pltpu.make_async_copy(view, view, b_sem.at[j, h, 1]).wait()
            part = jnp.dot(hidden[...], slots[s, h * down_rows:(h + 1) * down_rows, :],
                           preferred_element_type=f32)
            for c in range(tiles // 2):
                stage[pl.ds(h * (tiles // 2) + c, total, stride=tiles), :] = (
                    part[:, c * lanes:(c + 1) * lanes])
        rows = tok * tiles
        own_part[j] = stage[pl.ds(pl.multiple_of(me * rows, 8), rows), :]
        send_buf[j] = stage[...].reshape(peers, rows, lanes).astype(bf16)

        def push(k, carry):
            p = lax.rem(me + k, peers)
            remote(send_buf.at[j, p], recv_buf.at[j, me], rs_sem.at[j, p], rr_sem.at[j, me], p).start()
            return carry

        return lax.fori_loop(1, peers, push, carry)

    lax.fori_loop(0, chunks, down, 0)

    for j in range(chunks):
        def pull(k, acc):
            p = lax.rem(me + peers - k, peers)
            remote(send_buf.at[j, p], recv_buf.at[j, p], rs_sem.at[j, p], rr_sem.at[j, p], p).wait_recv()
            return acc + recv_buf[j, p].astype(f32)

        acc = lax.fori_loop(1, peers, pull, own_part[j])
        for r in range(tok):
            rows = slice(r * heads + j * tiles, r * heads + (j + 1) * tiles)
            rows_b[rows, :] = stream_v[rows, :] + acc[r * tiles:(r + 1) * tiles, :]
    out_ref[...] = rows_b[0:tok * heads, :].astype(bf16)

    def drain(k, carry):
        p = lax.rem(me + k, peers)
        remote(gathered.at[me], gathered.at[me], gs_sem.at[p], gr_sem.at[me], p).wait_send()
        remote(gates.at[me], gates.at[me], ts_sem.at[p], tr_sem.at[me], p).wait_send()
        for j in range(chunks):
            remote(send_buf.at[j, p], recv_buf.at[j, me], rs_sem.at[j, p], rr_sem.at[j, me], p).wait_send()
        return carry

    lax.fori_loop(1, peers, drain, 0)


def fused_fits(mesh, tok, shared_w, expert_w):
    peers = mesh.shape["grp"] * mesh.shape["sub"]
    chunk = 2 * shared_w
    return (peers > 1 and shared_w % 256 == 0 and expert_w % shared_w == 0
            and 2 * (shared_w + expert_w) <= D and D % chunk == 0
            and (KV_HEADS * HEAD) % shared_w == 0 and tok * (chunk // 128) % 16 == 0
            and (chunk // 128) % 8 == 0
            and (tok * EXPERTS) % 8 == 0 and tok * HEADS % 16 == 0 and EH % expert_w == 0
            and peers * tok <= 64)


def fused_call(mesh, *args):
    (query_rows, cache_keys, cache_values, residual, lengths, expert_ids, capacity, norm_gain,
     router, sg, su, sd, eg, eu, ed) = args
    tok = query_rows.shape[1]
    subs = mesh.shape["sub"]
    peers = mesh.shape["grp"] * subs
    width, expert_w = sg.shape[1], eg.shape[1]
    pairs = 1 + expert_w // width
    chunk = 2 * width
    chunks = D // chunk
    rows = tok * (chunk // 128)
    heads = D // 128
    total = peers * tok
    slot_count = 2 * pairs + 1
    f32, bf16 = jnp.float32, jnp.bfloat16
    V, DMA = pltpu.VMEM, pltpu.SemaphoreType.DMA
    kv = 2 * tok * (KV_HEADS * HEAD // width)
    out = pl.pallas_call(
        functools.partial(fused_layer, (subs, peers, tok)),
        out_shape=jax.ShapeDtypeStruct((tok * heads, 128), bf16),
        in_specs=[pl.BlockSpec(memory_space=pl.ANY)] * 15,
        out_specs=pl.BlockSpec(memory_space=pltpu.VMEM),
        scratch_shapes=[
            V((slot_count, D, width), bf16),
            V((1, tok, D), bf16), V((1, tok, D), bf16), V((EXPERTS, D), bf16), V((heads, 128), f32),
            pltpu.SMEM((1, tok), jnp.int32), pltpu.SMEM((1, tok), jnp.int32),
            pltpu.SMEM((EXPERTS,), jnp.int32),
            V((tok * heads + 8, 128), f32), V((tok * heads + 8, 128), f32), V((tok * heads, 128), f32),
            V((EXPERTS * heads, 128), f32),
            V((peers, tok * heads, 128), bf16), V((peers, tok * EXPERTS, 128), f32),
            V((peers * tok * heads, 128), f32), V((2, total, D), bf16),
            V((total, width + expert_w), bf16), V((total, width), f32),
            V((peers * rows, 128), f32), V((chunks, rows, 128), f32),
            V((chunks, peers, rows, 128), bf16), V((chunks, peers, rows, 128), bf16),
            DMA((7,)), DMA((kv,)), DMA((2 * pairs, 2)), DMA((chunks, 2, 2)),
            DMA((peers,)), DMA((peers,)), DMA((peers,)), DMA((peers,)),
            DMA((chunks, peers)), DMA((chunks, peers)),
        ],
        compiler_params=pltpu.CompilerParams(
            collective_id=0, has_side_effects=True, vmem_limit_bytes=67043328),
        name="fused_layer",
    )(query_rows, cache_keys, cache_values, residual, lengths, expert_ids.reshape(1, tok), capacity,
      norm_gain.reshape(heads, 128), router.T, sg, su, sd, eg, eu, ed)
    return out.reshape(1, tok, D)


def solution(mesh):
    placed = (
        P(("grp", "sub"), "rep", None),
        P(("grp", "sub"), "rep", None, None),
        P(("grp", "sub"), "rep", None, None),
        P(("grp", "sub"), "rep", None),
        P(("grp", "sub"), "rep"),
        P(("grp", "sub"), "rep", None),
        P(),
        P(),
        P(),
        P(None, ("grp", "sub")),
        P(None, ("grp", "sub")),
        P(("grp", "sub"), None),
        P(None, ("grp", "sub")),
        P(None, ("grp", "sub")),
        P(("grp", "sub"), None),
    )

    def body(*args):
        if fused_fits(mesh, args[0].shape[1], args[9].shape[1], args[12].shape[1]):
            return fused_call(mesh, *args)
        return per_device(*args)

    return jax.shard_map(
        body,
        mesh=mesh,
        in_specs=placed,
        out_specs=P(("grp", "sub"), "rep", None),
        check_vma=False,
    )
```

```python
import functools

import jax
import jax.numpy as jnp
from jax import lax
from jax.experimental import pallas as pl
from jax.experimental.pallas import tpu as pltpu
from jax.sharding import PartitionSpec as P

D = 5120
HEADS = 40
KV_HEADS = 8
HEAD = 128
EXPERTS = 4
EH = 8192


def attend(query_rows, cache_keys, cache_values, lengths):
    request_count = query_rows.shape[0]
    context = cache_keys.shape[1]
    groups = HEADS // KV_HEADS
    queries_f = query_rows.astype(jnp.float32).reshape(request_count, KV_HEADS, groups, HEAD)
    keys_f = cache_keys.astype(jnp.float32).reshape(request_count, context, KV_HEADS, HEAD)
    scores = jnp.einsum("rkgh,rjkh->rkgj", queries_f, keys_f) * HEAD ** (-0.5)
    key_pos = jnp.arange(context, dtype=jnp.int32)
    allowed = (key_pos[None, :] < lengths[:, None])[:, None, None, :]
    scores = jnp.where(allowed, scores, -1e30)
    row_peak = jnp.max(scores, axis=-1, keepdims=True)
    exponent = jnp.where(allowed, jnp.exp(scores - row_peak), 0.0)
    weights = (exponent / jnp.sum(exponent, axis=-1, keepdims=True)).astype(jnp.bfloat16)
    values_f = cache_values.astype(jnp.float32).reshape(request_count, context, KV_HEADS, HEAD)
    attended = jnp.einsum("rkgj,rjkh->rkgh", weights.astype(jnp.float32), values_f)
    return attended.reshape(request_count, HEADS * HEAD).astype(jnp.bfloat16)


def rms_normalize(stream, norm_gain):
    mean_square = jnp.mean(stream * stream, axis=-1, keepdims=True)
    return (stream * lax.rsqrt(mean_square + 1e-05) * norm_gain).astype(jnp.bfloat16)


def swiglu(inputs, w_gate, w_up, w_down):
    gate_part = jnp.dot(inputs, w_gate, preferred_element_type=jnp.float32)
    up_part = jnp.dot(inputs, w_up, preferred_element_type=jnp.float32)
    hidden = (jax.nn.silu(gate_part) * up_part).astype(jnp.bfloat16)
    return jnp.dot(hidden, w_down, preferred_element_type=jnp.float32)


def gated_inputs(flat_rows, router, route_ids):
    logits = jnp.dot(flat_rows, router, preferred_element_type=jnp.float32)
    onehot = route_ids[:, None] == jnp.arange(EXPERTS, dtype=jnp.int32)[None, :]
    picked = jnp.sum(jnp.where(onehot, logits, 0.0), axis=-1)
    return (flat_rows.astype(jnp.float32) * jax.nn.sigmoid(picked)[:, None]).astype(jnp.bfloat16)


def row_ranks(route_ids, capacity):
    onehot = (route_ids[:, None] == jnp.arange(EXPERTS, dtype=jnp.int32)[None, :]).astype(jnp.int32)
    before = jnp.cumsum(onehot, axis=0) - onehot
    row_rank = jnp.sum(before * onehot, axis=1)
    row_limit = jnp.sum(onehot * capacity[None, :], axis=1)
    return (row_rank, row_rank < row_limit)


def per_device(
    query_rows,
    cache_keys,
    cache_values,
    residual,
    lengths,
    expert_ids,
    capacity,
    norm_gain,
    router,
    shared_gate,
    shared_up,
    shared_down,
    expert_gate,
    expert_up,
    expert_down,
):
    tok_count = query_rows.shape[1]
    attended = attend(query_rows[0], cache_keys[0], cache_values[0], lengths[0])
    stream = residual[0].astype(jnp.float32) + attended.astype(jnp.float32)
    flat_rows = rms_normalize(stream, norm_gain)
    route_ids = expert_ids[0].reshape(tok_count)
    gathered, all_ids = (
        lax.all_gather(flat_rows, ("grp", "sub"), axis=0, tiled=True),
        lax.all_gather(route_ids, ("grp", "sub"), axis=0, tiled=True),
    )
    all_scaled = gated_inputs(gathered, router, all_ids)
    rank_unused, kept_all = jax.vmap(row_ranks, in_axes=(0, None))(
        all_ids.reshape(-1, tok_count), capacity
    )
    own_expert = lax.axis_index(("grp", "sub")) * expert_gate.shape[1] // EH
    usable = (all_ids == own_expert) & kept_all.reshape(-1)
    masked = jnp.where(usable[:, None], all_scaled, jnp.zeros_like(all_scaled))
    shared_part = swiglu(gathered, shared_gate, shared_up, shared_down)
    branch_sum = lax.psum_scatter(
        shared_part + swiglu(masked, expert_gate, expert_up, expert_down),
        ("grp", "sub"),
        scatter_dimension=0,
        tiled=True,
    )
    layer_out = stream + branch_sum
    return layer_out.astype(jnp.bfloat16).reshape(1, tok_count, D)


def fused_layer(sizes, *refs):
    (q_in, k_in, v_in, res_in, len_in, ids_in, cap_in, gain_in, router_in,
     sg_in, su_in, sd_in, eg_in, eu_in, ed_in, out_ref,
     slots, q_raw, res_raw, router_raw, gain_v, len_s, ids_s, cap_s,
     rows_a, rows_b, stream_v, router_f, gathered, gates, gathered_f, x_v, hidden, gate_part,
     stage, own_part, send_buf, recv_buf,
     small_sem, kv_sem, a_sem, b_sem, gs_sem, gr_sem, ts_sem, tr_sem, fs_sem, ft_sem,
     rs_sem, rr_sem) = refs
    subs, peers, tok = sizes
    width = slots.shape[2]
    depth = slots.shape[1]
    slot_count = slots.shape[0]
    lanes = 128
    heads = D // lanes
    groups = HEADS // KV_HEADS
    context = k_in.shape[2]
    shared_w, expert_w = sg_in.shape[1], eg_in.shape[1]
    pairs = 1 + expert_w // width
    half = depth // 2
    down_rows = shared_w + expert_w
    chunk = 2 * width
    chunks = D // chunk
    tiles = chunk // lanes
    total = peers * tok
    lag = min(2, chunks)
    f32, bf16 = jnp.float32, jnp.bfloat16

    rep = lax.axis_index("rep")
    me = lax.axis_index("grp") * subs + lax.axis_index("sub")

    def device(p):
        return (rep, p // subs, p % subs)

    small = [
        pltpu.make_async_copy(src, dst, small_sem.at[i])
        for i, (src, dst) in enumerate((
            (q_in, q_raw), (res_in, res_raw), (len_in, len_s), (ids_in, ids_s),
            (cap_in, cap_s), (gain_in, gain_v), (router_in, router_raw)))
    ]
    for copy in small:
        copy.start()

    kv_slot = slot_count - 1
    kv_cols = KV_HEADS * HEAD // width
    kv_copies = []
    for which, ref in enumerate((k_in, v_in)):
        for r in range(tok):
            for b in range(kv_cols):
                at = ((which * tok + r) * kv_cols + b)
                copy = pltpu.make_async_copy(
                    ref.at[0, r, :, pl.ds(b * width, width)],
                    slots.at[kv_slot, pl.ds(at * context, context), :],
                    kv_sem.at[at])
                copy.start()
                kv_copies.append(copy)

    def a_copy(s, h):
        p, up = s // 2, s % 2
        rows = pl.ds(h * half, half)
        if p == 0:
            src = (su_in if up else sg_in).at[rows, :]
        else:
            src = (eu_in if up else eg_in).at[rows, pl.ds((p - 1) * width, width)]
        return pltpu.make_async_copy(src, slots.at[s, rows, :], a_sem.at[s, h])

    def b_slot(j):
        return lax.rem(2 * pairs + j, slot_count)

    def b_start(j):
        s = (2 * pairs + j) % slot_count
        for h in range(2):
            cols = pl.ds(j * chunk + h * width, width)
            pltpu.make_async_copy(
                sd_in.at[:, cols], slots.at[s, pl.ds(h * down_rows, shared_w), :],
                b_sem.at[j, h, 0]).start(priority=1)
            pltpu.make_async_copy(
                ed_in.at[:, cols], slots.at[s, pl.ds(h * down_rows + shared_w, expert_w), :],
                b_sem.at[j, h, 1]).start(priority=1)

    for s in range(2 * pairs):
        for h in range(2):
            a_copy(s, h).start(priority=1)
    ahead = slot_count - 1 - 2 * pairs
    for j in range(ahead):
        b_start(j)

    barrier = pltpu.get_barrier_semaphore()

    def greet(k, carry):
        pl.semaphore_signal(barrier, inc=1, device_id=device(lax.rem(me + k, peers)),
                            device_id_type=pl.DeviceIdType.MESH)
        return carry

    lax.fori_loop(1, peers, greet, 0)

    for copy in small:
        copy.wait()
    rows_a[...] = jnp.zeros_like(rows_a)
    for c in range(heads):
        cols = pl.ds(c * lanes, lanes)
        rows_a[pl.ds(c, tok, stride=heads), :] = q_raw[0, :, cols].astype(f32)
        stream_v[pl.ds(c, tok, stride=heads), :] = res_raw[0, :, cols].astype(f32)
        router_f[pl.ds(c, EXPERTS, stride=heads), :] = router_raw[:, cols].astype(f32)
    for copy in kv_copies:
        copy.wait()

    def cache(which, r, g):
        b, inner = divmod(g * HEAD, width)
        at = (which * tok + r) * kv_cols + b
        return slots[kv_slot, at * context:(at + 1) * context, inner:inner + HEAD]

    for r in range(tok):
        for g in range(KV_HEADS):
            at = r * heads + g * groups
            rows_b[at:at + 8, :] = lax.dot_general(
                rows_a[at:at + 8, :].astype(bf16), cache(0, r, g),
                (((1,), (1,)), ((), ())), preferred_element_type=f32)
    scores = rows_b[0:tok * heads, :] * HEAD ** (-0.5)
    row_of = lax.broadcasted_iota(jnp.int32, scores.shape, 0)
    limit = jnp.full(scores.shape, len_s[0, 0], jnp.int32)
    for r in range(1, tok):
        limit = jnp.where(row_of >= r * heads, len_s[0, r], limit)
    allowed = lax.broadcasted_iota(jnp.int32, scores.shape, 1) < limit
    scores = jnp.where(allowed, scores, -1e30)
    exponent = jnp.where(allowed, jnp.exp(scores - jnp.max(scores, axis=1, keepdims=True)), 0.0)
    rows_a[0:tok * heads, :] = exponent / jnp.sum(exponent, axis=1, keepdims=True)
    for r in range(tok):
        for g in range(KV_HEADS):
            at = r * heads + g * groups
            rows_b[at:at + 8, :] = jnp.dot(
                rows_a[at:at + 8, :].astype(bf16), cache(1, r, g), preferred_element_type=f32)
    for j in range(ahead, min(ahead + 1, chunks)):
        b_start(j)
    stream = stream_v[...] + rows_b[0:tok * heads, :].astype(bf16).astype(f32)
    stream_v[...] = stream
    ids = [ids_s[0, r] for r in range(tok)]
    normed_rows = []
    for r in range(tok):
        part = stream[r * heads:(r + 1) * heads, :]
        square = jnp.sum(jnp.sum(part * part, axis=0, keepdims=True), axis=1, keepdims=True) / D
        normed_rows.append((part * lax.rsqrt(square + 1e-05) * gain_v[...]).astype(bf16))
    gathered[me] = jnp.concatenate([n.astype(f32) for n in normed_rows], axis=0).astype(bf16)
    gate_rows = []
    for r in range(tok):
        normed_f = normed_rows[r].astype(f32)
        picked = jnp.zeros((1, 1), f32)
        row_limit = jnp.int32(0)
        for e in range(EXPERTS):
            prod = normed_f * router_f[e * heads:(e + 1) * heads, :]
            logit = jnp.sum(jnp.sum(prod, axis=0, keepdims=True), axis=1, keepdims=True)
            match = (ids[r] == e).astype(jnp.int32)
            picked = picked + logit * match.astype(f32)
            row_limit = row_limit + match * cap_s[e]
        rank = jnp.int32(0)
        for b in range(r):
            rank = rank + (ids[b] == ids[r]).astype(jnp.int32)
        kept = (rank < row_limit).astype(jnp.int32)
        sig = jnp.broadcast_to(1.0 / (1.0 + jnp.exp(-picked)), (1, lanes))
        for e in range(EXPERTS):
            gate_rows.append(sig * (kept * (ids[r] == e).astype(jnp.int32)).astype(f32))
    gate_tile = jnp.concatenate(gate_rows, axis=0)
    gates[me] = gate_tile

    pl.semaphore_wait(barrier, peers - 1)

    def remote(src, dst, ssem, rsem, p):
        return pltpu.make_async_remote_copy(
            src_ref=src, dst_ref=dst, send_sem=ssem, recv_sem=rsem,
            device_id=device(p), device_id_type=pl.DeviceIdType.MESH)

    chips = peers // subs
    chip, sub = me // subs, lax.rem(me, subs)
    partners = [chip * subs + lax.rem(sub + o, subs) for o in range(1, subs)]

    def share(block, p, rows_sem, gate_sem):
        return (remote(gathered.at[block], gathered.at[block], rows_sem, gr_sem.at[block], p),
                remote(gates.at[block], gates.at[block], gate_sem, tr_sem.at[block], p))

    def own_share(p):
        return share(me, p, gs_sem.at[p], ts_sem.at[p])

    def ahead_chip(k):
        return lax.rem(chip + k, chips) * subs + sub

    def spread(k, carry):
        for copy in own_share(ahead_chip(k)):
            copy.start()
        return carry

    lax.fori_loop(1, chips, spread, 0)
    for p in partners:
        for copy in own_share(p):
            copy.start()
    rows_per = tok * heads

    def unpack(p):
        gathered_f[pl.ds(pl.multiple_of(p * rows_per, 8), rows_per), :] = gathered[p].astype(f32)

    unpack(me)

    def forward(block, o):
        return share(block, partners[o], fs_sem.at[block, o], ft_sem.at[block, o])

    def collect(k, carry):
        p = ahead_chip(chips - k)
        for copy in share(p, p, gs_sem.at[p], ts_sem.at[p]):
            copy.wait_recv()
        for o in range(subs - 1):
            for copy in forward(p, o):
                copy.start()
        unpack(p)
        return carry

    lax.fori_loop(1, chips, collect, 0)

    def collect_near(k, carry):
        for o in range(1, subs):
            p = lax.rem(chip + chips - k, chips) * subs + lax.rem(sub + o, subs)
            for copy in share(p, p, gs_sem.at[p], ts_sem.at[p]):
                copy.wait_recv()
            unpack(p)
        return carry

    lax.fori_loop(0, chips, collect_near, 0)

    own_expert = me * expert_w // EH
    gate_all = gates[...].reshape(peers * tok * EXPERTS, lanes)
    stage[0:peers * tok * EXPERTS, :] = gate_all
    gate = jnp.zeros((total, lanes), f32)
    for e in range(EXPERTS):
        mine = (own_expert == e).astype(f32)
        gate = gate + mine * stage[pl.ds(e, total, stride=EXPERTS), :]
    for c in range(heads):
        piece = gathered_f[pl.ds(c, total, stride=heads), :]
        x_v[0, :, c * lanes:(c + 1) * lanes] = piece.astype(bf16)
        x_v[1, :, c * lanes:(c + 1) * lanes] = (piece * gate).astype(bf16)

    def a_wait(s, h):
        view = slots.at[s, pl.ds(h * half, half), :]
        pltpu.make_async_copy(view, view, a_sem.at[s, h]).wait()

    def up_dot(s, which):
        a_wait(s, 0)
        first = jnp.dot(x_v[which, :, 0:half], slots[s, 0:half, :], preferred_element_type=f32)
        a_wait(s, 1)
        return first + jnp.dot(x_v[which, :, half:depth], slots[s, half:depth, :],
                               preferred_element_type=f32)

    def up_pair(p, carry):
        which = jnp.minimum(p, 1)
        gate_part[...] = up_dot(2 * p, which)
        up = up_dot(2 * p + 1, which)
        g = gate_part[...]
        hidden[:, pl.ds(pl.multiple_of(p * width, width), width)] = (
            g / (1.0 + jnp.exp(-g)) * up).astype(bf16)
        return carry

    issued = ahead + 1
    done = 0
    while issued < chunks:
        up_pair(done, 0)
        done += 1
        for j in range(issued, min(issued + 2, chunks)):
            b_start(j)
        issued = min(issued + 2, chunks)
    lax.fori_loop(done, pairs, up_pair, 0)

    def sent(k, carry):
        p = ahead_chip(k)
        for copy in own_share(p):
            copy.wait_send()
        for o in range(subs - 1):
            for copy in forward(p, o):
                copy.wait_send()
        return carry

    lax.fori_loop(1, chips, sent, 0)
    for p in partners:
        for copy in own_share(p):
            copy.wait_send()

    def finish(j):
        def pull(k, acc):
            p = lax.rem(me + peers - k, peers)
            copy = remote(send_buf.at[j, p], recv_buf.at[j, p], rs_sem.at[j, p], rr_sem.at[j, p], p)
            copy.wait_send()
            copy.wait_recv()
            return acc + recv_buf[j, p].astype(f32)

        acc = lax.fori_loop(1, peers, pull, own_part[j], unroll=True)
        for r in range(tok):
            rows = pl.ds(pl.multiple_of(r * heads + j * tiles, 8), tiles)
            rows_b[rows, :] = stream_v[rows, :] + acc[r * tiles:(r + 1) * tiles, :]

    def down(j, carry):
        s = b_slot(j)
        for h in range(2):
            view = slots.at[s, pl.ds(h * down_rows, shared_w), :]
            pltpu.make_async_copy(view, view, b_sem.at[j, h, 0]).wait()
            view = slots.at[s, pl.ds(h * down_rows + shared_w, expert_w), :]
            pltpu.make_async_copy(view, view, b_sem.at[j, h, 1]).wait()
            part = jnp.dot(hidden[...], slots[s, h * down_rows:(h + 1) * down_rows, :],
                           preferred_element_type=f32)
            for c in range(tiles // 2):
                stage[pl.ds(h * (tiles // 2) + c, total, stride=tiles), :] = (
                    part[:, c * lanes:(c + 1) * lanes])
        rows = tok * tiles
        own_part[j] = stage[pl.ds(pl.multiple_of(me * rows, 8), rows), :]
        send_buf[j] = stage[...].reshape(peers, rows, lanes).astype(bf16)

        def push(k, carry):
            p = lax.rem(me + k, peers)
            remote(send_buf.at[j, p], recv_buf.at[j, me], rs_sem.at[j, p], rr_sem.at[j, me], p).start()
            return carry

        lax.fori_loop(1, peers, push, 0, unroll=True)

        @pl.when(j >= lag)
        def _():
            finish(j - lag)

        return carry

    lax.fori_loop(0, chunks, down, 0)

    for j in range(chunks - lag, chunks):
        finish(j)
    out_ref[...] = rows_b[0:tok * heads, :].astype(bf16)


def fused_fits(mesh, tok, shared_w, expert_w):
    peers = mesh.shape["grp"] * mesh.shape["sub"]
    chunk = 2 * shared_w
    return (peers > 1 and shared_w % 256 == 0 and expert_w % shared_w == 0
            and 2 * (shared_w + expert_w) <= D and D % chunk == 0
            and (KV_HEADS * HEAD) % shared_w == 0 and tok * (chunk // 128) % 16 == 0
            and (chunk // 128) % 8 == 0
            and (tok * EXPERTS) % 8 == 0 and tok * HEADS % 16 == 0 and EH % expert_w == 0
            and peers * tok <= 64)


def fused_call(mesh, *args):
    (query_rows, cache_keys, cache_values, residual, lengths, expert_ids, capacity, norm_gain,
     router, sg, su, sd, eg, eu, ed) = args
    tok = query_rows.shape[1]
    subs = mesh.shape["sub"]
    peers = mesh.shape["grp"] * subs
    width, expert_w = sg.shape[1], eg.shape[1]
    pairs = 1 + expert_w // width
    chunk = 2 * width
    chunks = D // chunk
    rows = tok * (chunk // 128)
    heads = D // 128
    total = peers * tok
    slot_count = 2 * pairs + 1
    f32, bf16 = jnp.float32, jnp.bfloat16
    V, DMA = pltpu.VMEM, pltpu.SemaphoreType.DMA
    kv = 2 * tok * (KV_HEADS * HEAD // width)
    out = pl.pallas_call(
        functools.partial(fused_layer, (subs, peers, tok)),
        out_shape=jax.ShapeDtypeStruct((tok * heads, 128), bf16),
        in_specs=[pl.BlockSpec(memory_space=pl.ANY)] * 15,
        out_specs=pl.BlockSpec(memory_space=pltpu.VMEM),
        scratch_shapes=[
            V((slot_count, D, width), bf16),
            V((1, tok, D), bf16), V((1, tok, D), bf16), V((EXPERTS, D), bf16), V((heads, 128), f32),
            pltpu.SMEM((1, tok), jnp.int32), pltpu.SMEM((1, tok), jnp.int32),
            pltpu.SMEM((EXPERTS,), jnp.int32),
            V((tok * heads + 8, 128), f32), V((tok * heads + 8, 128), f32), V((tok * heads, 128), f32),
            V((EXPERTS * heads, 128), f32),
            V((peers, tok * heads, 128), bf16), V((peers, tok * EXPERTS, 128), f32),
            V((peers * tok * heads, 128), f32), V((2, total, D), bf16),
            V((total, width + expert_w), bf16), V((total, width), f32),
            V((peers * rows, 128), f32), V((chunks, rows, 128), f32),
            V((chunks, peers, rows, 128), bf16), V((chunks, peers, rows, 128), bf16),
            DMA((7,)), DMA((kv,)), DMA((2 * pairs, 2)), DMA((chunks, 2, 2)),
            DMA((peers,)), DMA((peers,)), DMA((peers,)), DMA((peers,)),
            DMA((peers, max(subs - 1, 1))), DMA((peers, max(subs - 1, 1))),
            DMA((chunks, peers)), DMA((chunks, peers)),
        ],
        compiler_params=pltpu.CompilerParams(
            collective_id=0, has_side_effects=True, vmem_limit_bytes=67043328),
        name="fused_layer",
    )(query_rows, cache_keys, cache_values, residual, lengths, expert_ids.reshape(1, tok), capacity,
      norm_gain.reshape(heads, 128), router.T, sg, su, sd, eg, eu, ed)
    return out.reshape(1, tok, D)


def solution(mesh):
    placed = (
        P(("grp", "sub"), "rep", None),
        P(("grp", "sub"), "rep", None, None),
        P(("grp", "sub"), "rep", None, None),
        P(("grp", "sub"), "rep", None),
        P(("grp", "sub"), "rep"),
        P(("grp", "sub"), "rep", None),
        P(),
        P(),
        P(),
        P(None, ("grp", "sub")),
        P(None, ("grp", "sub")),
        P(("grp", "sub"), None),
        P(None, ("grp", "sub")),
        P(None, ("grp", "sub")),
        P(("grp", "sub"), None),
    )

    def body(*args):
        if fused_fits(mesh, args[0].shape[1], args[9].shape[1], args[12].shape[1]):
            return fused_call(mesh, *args)
        return per_device(*args)

    return jax.shard_map(
        body,
        mesh=mesh,
        in_specs=placed,
        out_specs=P(("grp", "sub"), "rep", None),
        check_vma=False,
    )
```

```python
import functools

import jax
import jax.numpy as jnp
from jax import lax
from jax.experimental import pallas as pl
from jax.experimental.pallas import tpu as pltpu
from jax.sharding import PartitionSpec as P

D = 5120
HEADS = 40
KV_HEADS = 8
HEAD = 128
EXPERTS = 4
EH = 8192


def attend(query_rows, cache_keys, cache_values, lengths):
    request_count = query_rows.shape[0]
    context = cache_keys.shape[1]
    groups = HEADS // KV_HEADS
    queries_f = query_rows.astype(jnp.float32).reshape(request_count, KV_HEADS, groups, HEAD)
    keys_f = cache_keys.astype(jnp.float32).reshape(request_count, context, KV_HEADS, HEAD)
    scores = jnp.einsum("rkgh,rjkh->rkgj", queries_f, keys_f) * HEAD ** (-0.5)
    key_pos = jnp.arange(context, dtype=jnp.int32)
    allowed = (key_pos[None, :] < lengths[:, None])[:, None, None, :]
    scores = jnp.where(allowed, scores, -1e30)
    row_peak = jnp.max(scores, axis=-1, keepdims=True)
    exponent = jnp.where(allowed, jnp.exp(scores - row_peak), 0.0)
    weights = (exponent / jnp.sum(exponent, axis=-1, keepdims=True)).astype(jnp.bfloat16)
    values_f = cache_values.astype(jnp.float32).reshape(request_count, context, KV_HEADS, HEAD)
    attended = jnp.einsum("rkgj,rjkh->rkgh", weights.astype(jnp.float32), values_f)
    return attended.reshape(request_count, HEADS * HEAD).astype(jnp.bfloat16)


def rms_normalize(stream, norm_gain):
    mean_square = jnp.mean(stream * stream, axis=-1, keepdims=True)
    return (stream * lax.rsqrt(mean_square + 1e-05) * norm_gain).astype(jnp.bfloat16)


def swiglu(inputs, w_gate, w_up, w_down):
    gate_part = jnp.dot(inputs, w_gate, preferred_element_type=jnp.float32)
    up_part = jnp.dot(inputs, w_up, preferred_element_type=jnp.float32)
    hidden = (jax.nn.silu(gate_part) * up_part).astype(jnp.bfloat16)
    return jnp.dot(hidden, w_down, preferred_element_type=jnp.float32)


def gated_inputs(flat_rows, router, route_ids):
    logits = jnp.dot(flat_rows, router, preferred_element_type=jnp.float32)
    onehot = route_ids[:, None] == jnp.arange(EXPERTS, dtype=jnp.int32)[None, :]
    picked = jnp.sum(jnp.where(onehot, logits, 0.0), axis=-1)
    return (flat_rows.astype(jnp.float32) * jax.nn.sigmoid(picked)[:, None]).astype(jnp.bfloat16)


def row_ranks(route_ids, capacity):
    onehot = (route_ids[:, None] == jnp.arange(EXPERTS, dtype=jnp.int32)[None, :]).astype(jnp.int32)
    before = jnp.cumsum(onehot, axis=0) - onehot
    row_rank = jnp.sum(before * onehot, axis=1)
    row_limit = jnp.sum(onehot * capacity[None, :], axis=1)
    return (row_rank, row_rank < row_limit)


def per_device(
    query_rows,
    cache_keys,
    cache_values,
    residual,
    lengths,
    expert_ids,
    capacity,
    norm_gain,
    router,
    shared_gate,
    shared_up,
    shared_down,
    expert_gate,
    expert_up,
    expert_down,
):
    tok_count = query_rows.shape[1]
    attended = attend(query_rows[0], cache_keys[0], cache_values[0], lengths[0])
    stream = residual[0].astype(jnp.float32) + attended.astype(jnp.float32)
    flat_rows = rms_normalize(stream, norm_gain)
    route_ids = expert_ids[0].reshape(tok_count)
    gathered, all_ids = (
        lax.all_gather(flat_rows, ("grp", "sub"), axis=0, tiled=True),
        lax.all_gather(route_ids, ("grp", "sub"), axis=0, tiled=True),
    )
    all_scaled = gated_inputs(gathered, router, all_ids)
    rank_unused, kept_all = jax.vmap(row_ranks, in_axes=(0, None))(
        all_ids.reshape(-1, tok_count), capacity
    )
    own_expert = lax.axis_index(("grp", "sub")) * expert_gate.shape[1] // EH
    usable = (all_ids == own_expert) & kept_all.reshape(-1)
    masked = jnp.where(usable[:, None], all_scaled, jnp.zeros_like(all_scaled))
    shared_part = swiglu(gathered, shared_gate, shared_up, shared_down)
    branch_sum = lax.psum_scatter(
        shared_part + swiglu(masked, expert_gate, expert_up, expert_down),
        ("grp", "sub"),
        scatter_dimension=0,
        tiled=True,
    )
    layer_out = stream + branch_sum
    return layer_out.astype(jnp.bfloat16).reshape(1, tok_count, D)


def fused_layer(sizes, *refs):
    (q_in, k_in, v_in, res_in, len_in, ids_in, cap_in, gain_in, router_in,
     sg_in, su_in, sd_in, eg_in, eu_in, ed_in, out_ref,
     slots, q_raw, res_raw, router_raw, gain_v, len_s, ids_s, cap_s,
     rows_a, rows_b, stream_v, router_f, gathered, gates, gathered_f, x_v, hidden, gate_part,
     stage, own_part, send_buf, recv_buf,
     small_sem, kv_sem, a_sem, b_sem, gs_sem, gr_sem, ts_sem, tr_sem, fs_sem, ft_sem,
     rs_sem, rr_sem) = refs
    subs, peers, tok = sizes
    width = slots.shape[2]
    depth = slots.shape[1]
    slot_count = slots.shape[0]
    lanes = 128
    heads = D // lanes
    groups = HEADS // KV_HEADS
    context = k_in.shape[2]
    shared_w, expert_w = sg_in.shape[1], eg_in.shape[1]
    pairs = 1 + expert_w // width
    half = depth // 2
    down_rows = shared_w + expert_w
    chunk = 2 * width
    chunks = D // chunk
    tiles = chunk // lanes
    total = peers * tok
    lag = min(4, chunks)
    f32, bf16 = jnp.float32, jnp.bfloat16

    rep = lax.axis_index("rep")
    me = lax.axis_index("grp") * subs + lax.axis_index("sub")

    def device(p):
        return (rep, p // subs, p % subs)

    small = [
        pltpu.make_async_copy(src, dst, small_sem.at[i])
        for i, (src, dst) in enumerate((
            (q_in, q_raw), (res_in, res_raw), (len_in, len_s), (ids_in, ids_s),
            (cap_in, cap_s), (gain_in, gain_v), (router_in, router_raw)))
    ]
    for copy in small:
        copy.start()

    kv_slot = slot_count - 1
    kv_cols = KV_HEADS * HEAD // width
    kv_copies = []
    for which, ref in enumerate((k_in, v_in)):
        for r in range(tok):
            for b in range(kv_cols):
                at = ((which * tok + r) * kv_cols + b)
                copy = pltpu.make_async_copy(
                    ref.at[0, r, :, pl.ds(b * width, width)],
                    slots.at[kv_slot, pl.ds(at * context, context), :],
                    kv_sem.at[at])
                copy.start()
                kv_copies.append(copy)

    def a_copy(s, h):
        p, up = s // 2, s % 2
        rows = pl.ds(h * half, half)
        if p == 0:
            src = (su_in if up else sg_in).at[rows, :]
        else:
            src = (eu_in if up else eg_in).at[rows, pl.ds((p - 1) * width, width)]
        return pltpu.make_async_copy(src, slots.at[s, rows, :], a_sem.at[s, h])

    def b_slot(j):
        return lax.rem(2 * pairs + j, slot_count)

    def b_start(j):
        s = (2 * pairs + j) % slot_count
        for h in range(2):
            cols = pl.ds(j * chunk + h * width, width)
            pltpu.make_async_copy(
                sd_in.at[:, cols], slots.at[s, pl.ds(h * down_rows, shared_w), :],
                b_sem.at[j, h, 0]).start(priority=1)
            pltpu.make_async_copy(
                ed_in.at[:, cols], slots.at[s, pl.ds(h * down_rows + shared_w, expert_w), :],
                b_sem.at[j, h, 1]).start(priority=1)

    for s in range(2 * pairs):
        for h in range(2):
            a_copy(s, h).start(priority=1)
    ahead = slot_count - 1 - 2 * pairs
    for j in range(ahead):
        b_start(j)

    barrier = pltpu.get_barrier_semaphore()

    def greet(k, carry):
        pl.semaphore_signal(barrier, inc=1, device_id=device(lax.rem(me + k, peers)),
                            device_id_type=pl.DeviceIdType.MESH)
        return carry

    lax.fori_loop(1, peers, greet, 0)

    for copy in small:
        copy.wait()
    rows_a[...] = jnp.zeros_like(rows_a)
    for c in range(heads):
        cols = pl.ds(c * lanes, lanes)
        rows_a[pl.ds(c, tok, stride=heads), :] = q_raw[0, :, cols].astype(f32)
        stream_v[pl.ds(c, tok, stride=heads), :] = res_raw[0, :, cols].astype(f32)
        router_f[pl.ds(c, EXPERTS, stride=heads), :] = router_raw[:, cols].astype(f32)
    for copy in kv_copies:
        copy.wait()

    def cache(which, r, g):
        b, inner = divmod(g * HEAD, width)
        at = (which * tok + r) * kv_cols + b
        return slots[kv_slot, at * context:(at + 1) * context, inner:inner + HEAD]

    for r in range(tok):
        for g in range(KV_HEADS):
            at = r * heads + g * groups
            rows_b[at:at + 8, :] = lax.dot_general(
                rows_a[at:at + 8, :].astype(bf16), cache(0, r, g),
                (((1,), (1,)), ((), ())), preferred_element_type=f32)
    scores = rows_b[0:tok * heads, :] * HEAD ** (-0.5)
    row_of = lax.broadcasted_iota(jnp.int32, scores.shape, 0)
    limit = jnp.full(scores.shape, len_s[0, 0], jnp.int32)
    for r in range(1, tok):
        limit = jnp.where(row_of >= r * heads, len_s[0, r], limit)
    allowed = lax.broadcasted_iota(jnp.int32, scores.shape, 1) < limit
    scores = jnp.where(allowed, scores, -1e30)
    exponent = jnp.where(allowed, jnp.exp(scores - jnp.max(scores, axis=1, keepdims=True)), 0.0)
    rows_a[0:tok * heads, :] = exponent / jnp.sum(exponent, axis=1, keepdims=True)
    for r in range(tok):
        for g in range(KV_HEADS):
            at = r * heads + g * groups
            rows_b[at:at + 8, :] = jnp.dot(
                rows_a[at:at + 8, :].astype(bf16), cache(1, r, g), preferred_element_type=f32)
    for j in range(ahead, min(ahead + 1, chunks)):
        b_start(j)
    stream = stream_v[...] + rows_b[0:tok * heads, :].astype(bf16).astype(f32)
    stream_v[...] = stream
    ids = [ids_s[0, r] for r in range(tok)]
    normed_rows = []
    for r in range(tok):
        part = stream[r * heads:(r + 1) * heads, :]
        square = jnp.sum(jnp.sum(part * part, axis=0, keepdims=True), axis=1, keepdims=True) / D
        normed_rows.append((part * lax.rsqrt(square + 1e-05) * gain_v[...]).astype(bf16))
    gathered[me] = jnp.concatenate([n.astype(f32) for n in normed_rows], axis=0).astype(bf16)
    gate_rows = []
    for r in range(tok):
        normed_f = normed_rows[r].astype(f32)
        picked = jnp.zeros((1, 1), f32)
        row_limit = jnp.int32(0)
        for e in range(EXPERTS):
            prod = normed_f * router_f[e * heads:(e + 1) * heads, :]
            logit = jnp.sum(jnp.sum(prod, axis=0, keepdims=True), axis=1, keepdims=True)
            match = (ids[r] == e).astype(jnp.int32)
            picked = picked + logit * match.astype(f32)
            row_limit = row_limit + match * cap_s[e]
        rank = jnp.int32(0)
        for b in range(r):
            rank = rank + (ids[b] == ids[r]).astype(jnp.int32)
        kept = (rank < row_limit).astype(jnp.int32)
        sig = jnp.broadcast_to(1.0 / (1.0 + jnp.exp(-picked)), (1, lanes))
        for e in range(EXPERTS):
            gate_rows.append(sig * (kept * (ids[r] == e).astype(jnp.int32)).astype(f32))
    gate_tile = jnp.concatenate(gate_rows, axis=0)
    gates[me] = gate_tile

    pl.semaphore_wait(barrier, peers - 1)

    def remote(src, dst, ssem, rsem, p):
        return pltpu.make_async_remote_copy(
            src_ref=src, dst_ref=dst, send_sem=ssem, recv_sem=rsem,
            device_id=device(p), device_id_type=pl.DeviceIdType.MESH)

    chips = peers // subs
    chip, sub = me // subs, lax.rem(me, subs)
    partners = [chip * subs + lax.rem(sub + o, subs) for o in range(1, subs)]

    def share(block, p, rows_sem, gate_sem):
        return (remote(gathered.at[block], gathered.at[block], rows_sem, gr_sem.at[block], p),
                remote(gates.at[block], gates.at[block], gate_sem, tr_sem.at[block], p))

    def own_share(p):
        return share(me, p, gs_sem.at[p], ts_sem.at[p])

    def ahead_chip(k):
        return lax.rem(chip + k, chips) * subs + sub

    def spread(k, carry):
        for copy in own_share(ahead_chip(k)):
            copy.start()
        return carry

    lax.fori_loop(1, chips, spread, 0)
    for p in partners:
        for copy in own_share(p):
            copy.start()
    rows_per = tok * heads

    def unpack(p):
        gathered_f[pl.ds(pl.multiple_of(p * rows_per, 8), rows_per), :] = gathered[p].astype(f32)

    unpack(me)

    def forward(block, o):
        return share(block, partners[o], fs_sem.at[block, o], ft_sem.at[block, o])

    def collect(k, carry):
        p = ahead_chip(chips - k)
        for copy in share(p, p, gs_sem.at[p], ts_sem.at[p]):
            copy.wait_recv()
        for o in range(subs - 1):
            for copy in forward(p, o):
                copy.start()
        unpack(p)
        return carry

    lax.fori_loop(1, chips, collect, 0)

    def collect_near(k, carry):
        for o in range(1, subs):
            p = lax.rem(chip + chips - k, chips) * subs + lax.rem(sub + o, subs)
            for copy in share(p, p, gs_sem.at[p], ts_sem.at[p]):
                copy.wait_recv()
            unpack(p)
        return carry

    lax.fori_loop(0, chips, collect_near, 0)

    own_expert = me * expert_w // EH
    gate_all = gates[...].reshape(peers * tok * EXPERTS, lanes)
    stage[0:peers * tok * EXPERTS, :] = gate_all
    gate = jnp.zeros((total, lanes), f32)
    for e in range(EXPERTS):
        mine = (own_expert == e).astype(f32)
        gate = gate + mine * stage[pl.ds(e, total, stride=EXPERTS), :]
    for c in range(heads):
        piece = gathered_f[pl.ds(c, total, stride=heads), :]
        x_v[0, :, c * lanes:(c + 1) * lanes] = piece.astype(bf16)
        x_v[1, :, c * lanes:(c + 1) * lanes] = (piece * gate).astype(bf16)

    def a_wait(s, h):
        view = slots.at[s, pl.ds(h * half, half), :]
        pltpu.make_async_copy(view, view, a_sem.at[s, h]).wait()

    def up_dot(s, which):
        a_wait(s, 0)
        first = jnp.dot(x_v[which, :, 0:half], slots[s, 0:half, :], preferred_element_type=f32)
        a_wait(s, 1)
        return first + jnp.dot(x_v[which, :, half:depth], slots[s, half:depth, :],
                               preferred_element_type=f32)

    def up_pair(p, carry):
        which = jnp.minimum(p, 1)
        gate_part[...] = up_dot(2 * p, which)
        up = up_dot(2 * p + 1, which)
        g = gate_part[...]
        hidden[:, pl.ds(pl.multiple_of(p * width, width), width)] = (
            g / (1.0 + jnp.exp(-g)) * up).astype(bf16)
        return carry

    issued = ahead + 1
    done = 0
    while issued < chunks:
        up_pair(done, 0)
        done += 1
        for j in range(issued, min(issued + 2, chunks)):
            b_start(j)
        issued = min(issued + 2, chunks)
    lax.fori_loop(done, pairs, up_pair, 0)

    def sent(k, carry):
        p = ahead_chip(k)
        for copy in own_share(p):
            copy.wait_send()
        for o in range(subs - 1):
            for copy in forward(p, o):
                copy.wait_send()
        return carry

    lax.fori_loop(1, chips, sent, 0)
    for p in partners:
        for copy in own_share(p):
            copy.wait_send()

    def finish(j):
        def pull(k, acc):
            p = lax.rem(me + peers - k, peers)
            copy = remote(send_buf.at[j, p], recv_buf.at[j, p], rs_sem.at[j, p], rr_sem.at[j, p], p)
            copy.wait_send()
            copy.wait_recv()
            return acc + recv_buf[j, p].astype(f32)

        acc = lax.fori_loop(1, peers, pull, own_part[j], unroll=True)
        for r in range(tok):
            rows = pl.ds(pl.multiple_of(r * heads + j * tiles, 8), tiles)
            rows_b[rows, :] = stream_v[rows, :] + acc[r * tiles:(r + 1) * tiles, :]

    def down(j, carry):
        s = b_slot(j)
        for h in range(2):
            view = slots.at[s, pl.ds(h * down_rows, shared_w), :]
            pltpu.make_async_copy(view, view, b_sem.at[j, h, 0]).wait()
            view = slots.at[s, pl.ds(h * down_rows + shared_w, expert_w), :]
            pltpu.make_async_copy(view, view, b_sem.at[j, h, 1]).wait()
            part = jnp.dot(hidden[...], slots[s, h * down_rows:(h + 1) * down_rows, :],
                           preferred_element_type=f32)
            for c in range(tiles // 2):
                stage[pl.ds(h * (tiles // 2) + c, total, stride=tiles), :] = (
                    part[:, c * lanes:(c + 1) * lanes])
        rows = tok * tiles
        own_part[j] = stage[pl.ds(pl.multiple_of(me * rows, 8), rows), :]
        send_buf[j] = stage[...].reshape(peers, rows, lanes).astype(bf16)

        def push(k, carry):
            p = lax.rem(me + k, peers)
            remote(send_buf.at[j, p], recv_buf.at[j, me], rs_sem.at[j, p], rr_sem.at[j, me], p).start()
            return carry

        lax.fori_loop(1, peers, push, 0, unroll=True)

        @pl.when(j >= lag)
        def _():
            finish(j - lag)

        return carry

    lax.fori_loop(0, chunks, down, 0)

    for j in range(chunks - lag, chunks):
        finish(j)
    out_ref[...] = rows_b[0:tok * heads, :].astype(bf16)


def fused_fits(mesh, tok, shared_w, expert_w):
    peers = mesh.shape["grp"] * mesh.shape["sub"]
    chunk = 2 * shared_w
    return (peers > 1 and shared_w % 256 == 0 and expert_w % shared_w == 0
            and 2 * (shared_w + expert_w) <= D and D % chunk == 0
            and (KV_HEADS * HEAD) % shared_w == 0 and tok * (chunk // 128) % 16 == 0
            and (chunk // 128) % 8 == 0
            and (tok * EXPERTS) % 8 == 0 and tok * HEADS % 16 == 0 and EH % expert_w == 0
            and peers * tok <= 64)


def fused_call(mesh, *args):
    (query_rows, cache_keys, cache_values, residual, lengths, expert_ids, capacity, norm_gain,
     router, sg, su, sd, eg, eu, ed) = args
    tok = query_rows.shape[1]
    subs = mesh.shape["sub"]
    peers = mesh.shape["grp"] * subs
    width, expert_w = sg.shape[1], eg.shape[1]
    pairs = 1 + expert_w // width
    chunk = 2 * width
    chunks = D // chunk
    rows = tok * (chunk // 128)
    heads = D // 128
    total = peers * tok
    slot_count = 2 * pairs + 1
    f32, bf16 = jnp.float32, jnp.bfloat16
    V, DMA = pltpu.VMEM, pltpu.SemaphoreType.DMA
    kv = 2 * tok * (KV_HEADS * HEAD // width)
    out = pl.pallas_call(
        functools.partial(fused_layer, (subs, peers, tok)),
        out_shape=jax.ShapeDtypeStruct((tok * heads, 128), bf16),
        in_specs=[pl.BlockSpec(memory_space=pl.ANY)] * 15,
        out_specs=pl.BlockSpec(memory_space=pltpu.VMEM),
        scratch_shapes=[
            V((slot_count, D, width), bf16),
            V((1, tok, D), bf16), V((1, tok, D), bf16), V((EXPERTS, D), bf16), V((heads, 128), f32),
            pltpu.SMEM((1, tok), jnp.int32), pltpu.SMEM((1, tok), jnp.int32),
            pltpu.SMEM((EXPERTS,), jnp.int32),
            V((tok * heads + 8, 128), f32), V((tok * heads + 8, 128), f32), V((tok * heads, 128), f32),
            V((EXPERTS * heads, 128), f32),
            V((peers, tok * heads, 128), bf16), V((peers, tok * EXPERTS, 128), f32),
            V((peers * tok * heads, 128), f32), V((2, total, D), bf16),
            V((total, width + expert_w), bf16), V((total, width), f32),
            V((peers * rows, 128), f32), V((chunks, rows, 128), f32),
            V((chunks, peers, rows, 128), bf16), V((chunks, peers, rows, 128), bf16),
            DMA((7,)), DMA((kv,)), DMA((2 * pairs, 2)), DMA((chunks, 2, 2)),
            DMA((peers,)), DMA((peers,)), DMA((peers,)), DMA((peers,)),
            DMA((peers, max(subs - 1, 1))), DMA((peers, max(subs - 1, 1))),
            DMA((chunks, peers)), DMA((chunks, peers)),
        ],
        compiler_params=pltpu.CompilerParams(
            collective_id=0, has_side_effects=True, vmem_limit_bytes=67043328),
        name="fused_layer",
    )(query_rows, cache_keys, cache_values, residual, lengths, expert_ids.reshape(1, tok), capacity,
      norm_gain.reshape(heads, 128), router.T, sg, su, sd, eg, eu, ed)
    return out.reshape(1, tok, D)


def solution(mesh):
    placed = (
        P(("grp", "sub"), "rep", None),
        P(("grp", "sub"), "rep", None, None),
        P(("grp", "sub"), "rep", None, None),
        P(("grp", "sub"), "rep", None),
        P(("grp", "sub"), "rep"),
        P(("grp", "sub"), "rep", None),
        P(),
        P(),
        P(),
        P(None, ("grp", "sub")),
        P(None, ("grp", "sub")),
        P(("grp", "sub"), None),
        P(None, ("grp", "sub")),
        P(None, ("grp", "sub")),
        P(("grp", "sub"), None),
    )

    def body(*args):
        if fused_fits(mesh, args[0].shape[1], args[9].shape[1], args[12].shape[1]):
            return fused_call(mesh, *args)
        return per_device(*args)

    return jax.shard_map(
        body,
        mesh=mesh,
        in_specs=placed,
        out_specs=P(("grp", "sub"), "rep", None),
        check_vma=False,
    )
```
